32 devices in a mesh: bank: 8 (over z, y), feat: 4 (over x, core).
Axes of the slice: x: 2, y: 2, z: 4, core: 2. Of those that a mesh axis runs over, the one named last changes fastest.
Arguments:
- bank_rows: bfloat16 [12288, 1536], P('bank', 'feat'), may hold values from -16 to 16
- offsets: int32 [17], replicated, may hold values from 0 to 24576, as said below
Outputs:
- whitened: bfloat16 [12288, 1536], P('bank', 'feat')
The draws below stay inside these ranges and needn't reach their ends.
Inputs may be any that keep to these rules, and one draw needn't show every extreme that they name: offsets[0] = 0 and offsets[16] = 24576; cluster k holds the rows offsets[k] to offsets[k+1] - 1, and every cluster holds 1152 to 1920 rows, both counts reached in every draw.
All inputs are finite; a program needn't handle non-finite values.
Results may differ from the reference program's by a relative error of at most 0.0058.
Values may be sent and summed in bfloat16 or wider, within the bound.
A program may use at most 128 MiB of HBM per device.

```python
import jax
import jax.numpy as jnp
from jax import lax

D = 768
ROWS_DEV = 3072
ROWS = 24576
CLUSTERS = 16


def draw_offsets(key, part):
    size_key, order_key = jax.random.split(key)
    half_rows = ROWS_DEV // 2
    spread_rows = ROWS_DEV // 8
    deviation = jax.random.randint(size_key, (CLUSTERS // 2,), 0, spread_rows + 1, dtype=jnp.int32)
    deviation = deviation.at[0].set(spread_rows)
    row_counts = jnp.stack([half_rows + deviation, half_rows - deviation], axis=1).reshape(-1)
    shuffle = jax.random.permutation(order_key, CLUSTERS)
    row_counts = row_counts[shuffle]
    return jnp.concatenate([jnp.zeros((1,), jnp.int32), jnp.cumsum(row_counts).astype(jnp.int32)])


def draw_bank_rows(key, part):
    noise_key, scale_key = jax.random.split(key)
    noise_values = jnp.clip(jax.random.normal(noise_key, (ROWS, D), jnp.float32), -5.0, 5.0)
    scales = jnp.exp(jax.random.uniform(scale_key, (1, D), jnp.float32, jnp.log(0.5), jnp.log(2.0)))
    mixed = noise_values + 0.6 * jnp.roll(noise_values, 1, axis=1)
    return (scales * mixed).astype(jnp.bfloat16).reshape(ROWS // 2, 2 * D)


def setup_inputs(seed: int = 0) -> dict:
    streams_of = jax.random.split(jax.random.key(seed), 3)
    bank_rows = draw_bank_rows(jax.random.fold_in(streams_of[2], 71), 0)
    offsets = draw_offsets(jax.random.fold_in(streams_of[2], 71), 0)
    return {"bank_rows": bank_rows, "offsets": offsets}


ridge_shift = 0.5

def transposed_product(left_rows, right_rows):
    return lax.dot_general(left_rows.astype(jnp.float32), right_rows.astype(jnp.float32), (((0,), (0,)), ((), ())), preferred_element_type=jnp.float32)

def add_slot(gram_tiles, term, slot_index):
    current = lax.dynamic_index_in_dim(gram_tiles, slot_index, 0, keepdims=False)
    return lax.dynamic_update_index_in_dim(gram_tiles, current + term, slot_index, 0)

def reference(bank_rows, offsets):
    full_width = bank_rows.shape[1] // 2
    total_rows = bank_rows.shape[0] * 2
    flat_rows = bank_rows.reshape(total_rows, full_width)
    cluster_count = offsets.shape[0] - 1
    block_rows = min(512, ROWS_DEV // 4)
    boundaries = offsets[1:-1]

    def labels_of(offset_row):
        positions = offset_row + jnp.arange(block_rows, dtype=jnp.int32)
        return jnp.sum((boundaries[None, :] <= positions[:, None]).astype(jnp.int32), axis=1)

    def split_rows(offset_row):
        block_data = lax.dynamic_slice_in_dim(flat_rows, offset_row, block_rows, 0)
        block_labels = labels_of(offset_row)
        lead_label = block_labels[0]
        later_mask = (block_labels != lead_label).astype(jnp.bfloat16)[:, None]
        later_rows = block_data * later_mask
        early_rows = block_data - later_rows
        return (block_data, early_rows, later_rows, lead_label)

    def gram_step(gram_tiles, offset_row):
        block_data, early_rows, later_rows, lead_label = split_rows(offset_row)
        gram_tiles = add_slot(gram_tiles, transposed_product(early_rows, block_data), lead_label)
        gram_tiles = add_slot(gram_tiles, transposed_product(later_rows, block_data), jnp.minimum(lead_label + 1, cluster_count - 1))
        return (gram_tiles, None)
    block_starts = jnp.arange(total_rows // block_rows, dtype=jnp.int32) * block_rows
    gram_tiles, _ = lax.scan(gram_step, jnp.zeros((cluster_count, full_width, full_width), jnp.float32), block_starts)
    row_counts = (offsets[1:] - offsets[:-1]).astype(jnp.float32)
    identity = jnp.eye(full_width, dtype=jnp.float32)
    covariance = gram_tiles / row_counts[:, None, None] + ridge_shift * identity
    factor = jnp.linalg.cholesky(covariance)
    inverse = lax.linalg.triangular_solve(factor, jnp.broadcast_to(identity, covariance.shape), left_side=True, lower=True)
    whitener = inverse.astype(jnp.bfloat16)

    def whiten_step(carry, offset_row):
        block_data, early_rows, later_rows, lead_label = split_rows(offset_row)
        first_factor = lax.dynamic_index_in_dim(whitener, lead_label, 0, keepdims=False)
        second_factor = lax.dynamic_index_in_dim(whitener, jnp.minimum(lead_label + 1, cluster_count - 1), 0, keepdims=False)
        product_rows = lax.dot_general(early_rows.astype(jnp.float32), first_factor.astype(jnp.float32), (((1,), (1,)), ((), ())), preferred_element_type=jnp.float32)
        product_rows = product_rows + lax.dot_general(later_rows.astype(jnp.float32), second_factor.astype(jnp.float32), (((1,), (1,)), ((), ())), preferred_element_type=jnp.float32)
        return (carry, product_rows.astype(jnp.bfloat16))
    _, pieces = lax.scan(whiten_step, jnp.int32(0), block_starts)
    return pieces.reshape(total_rows // 2, 2 * full_width)
```

```python
import jax
import jax.numpy as jnp
from jax import lax
from jax.experimental import pallas as pl
from jax.experimental.pallas import tpu as pltpu
from jax.sharding import PartitionSpec as P

TOUCH = 4
BLOCK = 128
SUB = 8
ridge_shift = 0.5


def slot_bounds(offsets, row_start, rows_dev):
    boundaries = offsets[1:-1]
    first_label = jnp.sum((boundaries <= row_start).astype(jnp.int32))
    last_label = jnp.sum((boundaries <= row_start + rows_dev - 1).astype(jnp.int32))
    roles = jnp.arange(TOUCH, dtype=jnp.int32)
    labels = jnp.where(
        roles == TOUCH - 1, last_label, jnp.minimum(first_label + roles, last_label)
    )
    used = jnp.logical_or(roles == TOUCH - 1, first_label + roles < last_label)
    low = jnp.clip(offsets[labels] - row_start, 0, rows_dev)
    high = jnp.clip(offsets[labels + 1] - row_start, 0, rows_dev)
    high = jnp.where(used, high, low)
    counts = offsets[labels + 1] - offsets[labels]
    return low, high, counts, first_label, last_label


def gram_kernel(bounds, pairs_ref, gram_ref):
    step = pl.program_id(0)
    block_pairs = pairs_ref.shape[0]
    width = pairs_ref.shape[1] // 2
    low, high = bounds[0], bounds[1]
    start = step * block_pairs * 2

    @pl.when(step == 0)
    def _():
        gram_ref[...] = jnp.zeros_like(gram_ref)

    @pl.when(jnp.logical_and(start < high, start + 2 * block_pairs > low))
    def _():
        row = start + 2 * lax.broadcasted_iota(jnp.int32, (block_pairs, 1), 0)
        for parity in range(2):
            data = pairs_ref[:, parity * width : (parity + 1) * width]
            keep = jnp.logical_and(row + parity >= low, row + parity < high)
            data = jnp.where(keep, data, jnp.zeros_like(data))
            gram_ref[...] += lax.dot_general(
                data, data, (((0,), (0,)), ((), ())), preferred_element_type=jnp.float32
            )


def own_gram(pairs, bounds):
    pair_rows, pair_width = pairs.shape
    width = pair_width // 2
    block_pairs = min(256, pair_rows)
    return pl.pallas_call(
        gram_kernel,
        grid_spec=pltpu.PrefetchScalarGridSpec(
            num_scalar_prefetch=1,
            grid=(pair_rows // block_pairs,),
            in_specs=[pl.BlockSpec((block_pairs, pair_width), lambda i, b: (i, 0))],
            out_specs=pl.BlockSpec((width, width), lambda i, b: (0, 0)),
        ),
        out_shape=jax.ShapeDtypeStruct((width, width), jnp.float32),
        compiler_params=pltpu.CompilerParams(vmem_limit_bytes=32 << 20),
    )(bounds, pairs)


def split_rows(value):
    high = value.astype(jnp.bfloat16).astype(jnp.float32)
    rest = value - high
    middle = rest.astype(jnp.bfloat16).astype(jnp.float32)
    low = (rest - middle).astype(jnp.bfloat16).astype(jnp.float32)
    return high, middle, low


def factor_block(work):
    for panel in range(BLOCK // SUB):
        base = panel * SUB
        rows = [work[base + i : base + i + 1, :] for i in range(SUB)]
        entry = {}
        for i in range(SUB):
            for k in range(i, SUB):
                column = base + k
                entry[i, k] = jnp.broadcast_to(rows[i][:, column : column + 1], (1, BLOCK))
        done = []
        for i in range(SUB):
            inverse_root = lax.rsqrt(entry[i, i])
            coefficient = {k: entry[i, k] * inverse_root for k in range(i + 1, SUB)}
            for k in range(i + 1, SUB):
                for m in range(k, SUB):
                    entry[k, m] = entry[k, m] - coefficient[k] * coefficient[m]
            scaled = rows[i] * jnp.concatenate([inverse_root, inverse_root], axis=1)
            done.append(scaled)
            for k in range(i + 1, SUB):
                both = jnp.concatenate([coefficient[k], coefficient[k]], axis=1)
                rows[k] = rows[k] - both * scaled
        for i in range(SUB):
            work[base + i : base + i + 1, :] = done[i]
        if base + SUB < BLOCK:
            high, middle, low = split_rows(work[base : base + SUB, :])
            left = jnp.concatenate([high, high, middle, high, middle, low], axis=0)
            right = jnp.concatenate([high, middle, high, low, middle, high], axis=0)
            update = lax.dot_general(
                left[:, :BLOCK].astype(jnp.bfloat16),
                right.astype(jnp.bfloat16),
                (((0,), (0,)), ((), ())),
                preferred_element_type=jnp.float32,
            )
            work[base + SUB :, :] = work[base + SUB :, :] - update[base + SUB :, :]


def whitener_kernel(scalars, own_ref, other_ref, out_ref, matrix, work):
    width = own_ref.shape[0]
    blocks = width // BLOCK
    joined = scalars[0] > 0
    count = scalars[1].astype(jnp.float32)
    eye = (
        lax.broadcasted_iota(jnp.int32, (BLOCK, BLOCK), 0)
        == lax.broadcasted_iota(jnp.int32, (BLOCK, BLOCK), 1)
    ).astype(jnp.float32)
    for i in range(blocks):
        span = slice(i * BLOCK, (i + 1) * BLOCK)
        total = own_ref[span, :] + jnp.where(joined, other_ref[span, :], 0.0)
        matrix[span, :width] = total / count
        matrix[span, width:] = jnp.zeros((BLOCK, width), jnp.float32)
    for i in range(blocks):
        span = slice(i * BLOCK, (i + 1) * BLOCK)
        matrix[span, span] = matrix[span, span] + ridge_shift * eye
        matrix[span, width + i * BLOCK : width + (i + 1) * BLOCK] = eye

    @pl.loop(0, blocks)
    def _(j):
        here = pl.multiple_of(j * BLOCK, BLOCK)
        work[:, :BLOCK] = matrix[pl.ds(here, BLOCK), pl.ds(here, BLOCK)]
        work[:, BLOCK:] = eye
        factor_block(work)
        panel = lax.dot_general(
            work[:, BLOCK:],
            matrix[pl.ds(here, BLOCK), :],
            (((1,), (0,)), ((), ())),
            precision=lax.Precision.HIGHEST,
            preferred_element_type=jnp.float32,
        )
        matrix[pl.ds(here, BLOCK), :] = panel

        @pl.loop(j + 1, blocks)
        def _(i):
            there = pl.multiple_of(i * BLOCK, BLOCK)
            update = lax.dot_general(
                matrix[pl.ds(here, BLOCK), pl.ds(there, BLOCK)],
                matrix[pl.ds(here, BLOCK), :],
                (((0,), (0,)), ((), ())),
                precision=lax.Precision.HIGHEST,
                preferred_element_type=jnp.float32,
            )
            matrix[pl.ds(there, BLOCK), :] = matrix[pl.ds(there, BLOCK), :] - update

    out_ref[...] = matrix[:, width:].astype(jnp.bfloat16)


def own_whitener(scalars, own, other):
    width = own.shape[0]
    return pl.pallas_call(
        whitener_kernel,
        in_specs=[
            pl.BlockSpec(memory_space=pltpu.SMEM),
            pl.BlockSpec(memory_space=pltpu.VMEM),
            pl.BlockSpec(memory_space=pltpu.VMEM),
        ],
        out_specs=pl.BlockSpec(memory_space=pltpu.VMEM),
        out_shape=jax.ShapeDtypeStruct((width, width), jnp.bfloat16),
        scratch_shapes=[
            pltpu.VMEM((width, 2 * width), jnp.float32),
            pltpu.VMEM((BLOCK, 2 * BLOCK), jnp.float32),
        ],
        compiler_params=pltpu.CompilerParams(vmem_limit_bytes=40 << 20),
    )(scalars, own, other)


def whiten_kernel(scalars, rows_ref, factor_ref, out_ref, total):
    step = pl.program_id(0)
    block_pairs = rows_ref.shape[0]
    parity = scalars[0]
    start = step * block_pairs * 2
    row = start + parity + 2 * lax.broadcasted_iota(jnp.int32, (block_pairs, 1), 0)
    total[...] = jnp.zeros_like(total)
    for role in range(TOUCH):
        low, high, place = scalars[1 + role], scalars[1 + TOUCH + role], scalars[1 + 2 * TOUCH + role]

        @pl.when(jnp.logical_and(start < high, start + 2 * block_pairs > low))
        def _():
            data = rows_ref[...]
            keep = jnp.logical_and(row >= low, row < high)
            data = jnp.where(keep, data, jnp.zeros_like(data))
            total[...] += lax.dot_general(
                data, factor_ref[place], (((1,), (1,)), ((), ())), preferred_element_type=jnp.float32
            )

    out_ref[...] = total[...].astype(jnp.bfloat16)


def whiten(scalars, pairs, factor_rows):
    pair_rows, pair_width = pairs.shape
    width = pair_width // 2
    out_width = factor_rows.shape[1]
    block_pairs = min(256, pair_rows)
    return pl.pallas_call(
        whiten_kernel,
        grid_spec=pltpu.PrefetchScalarGridSpec(
            num_scalar_prefetch=1,
            grid=(pair_rows // block_pairs,),
            in_specs=[
                pl.BlockSpec((block_pairs, width), lambda i, s: (i, s[0])),
                pl.BlockSpec(factor_rows.shape, lambda i, s: (0, 0, 0)),
            ],
            out_specs=pl.BlockSpec((block_pairs, out_width), lambda i, s: (i, 0)),
            scratch_shapes=[pltpu.VMEM((block_pairs, out_width), jnp.float32)],
        ),
        out_shape=jax.ShapeDtypeStruct((pair_rows, out_width), jnp.bfloat16),
        compiler_params=pltpu.CompilerParams(vmem_limit_bytes=32 << 20),
    )(scalars, pairs, factor_rows)


def meeting_pairs(bank_count, feat_count):
    pairs = []
    for bank in range(bank_count - 1):
        place = feat_count - 1 if bank % 2 == 0 else 0
        left, right = bank * feat_count + place, (bank + 1) * feat_count + place
        pairs += [(left, right), (right, left)]
    return pairs


def shards(bank_rows, offsets):
    pair_rows, out_width = bank_rows.shape
    rows_dev = pair_rows * 2
    bank, feat = lax.axis_index("bank"), lax.axis_index("feat")
    bank_count, feat_count = lax.axis_size("bank"), lax.axis_size("feat")
    pairs = lax.all_gather(bank_rows, "feat", axis=1, tiled=True)
    full_width = pairs.shape[1] // 2
    row_start = bank * rows_dev
    low, high, counts, first_label, last_label = slot_bounds(offsets, row_start, rows_dev)
    roles = jnp.arange(TOUCH, dtype=jnp.int32)
    places = jnp.where(bank % 2 == 0, roles, TOUCH - 1 - roles)
    role = jnp.where(bank % 2 == 0, feat, TOUCH - 1 - feat)
    own = own_gram(pairs, jnp.stack([low[role], high[role]]))
    other = lax.ppermute(own, ("bank", "feat"), meeting_pairs(bank_count, feat_count))
    left_open = offsets[first_label] < row_start
    right_open = offsets[last_label + 1] > row_start + rows_dev
    joined = jnp.logical_or(
        jnp.logical_and(role == 0, left_open), jnp.logical_and(role == TOUCH - 1, right_open)
    )
    inverse = own_whitener(jnp.stack([joined.astype(jnp.int32), counts[role]]), own, other)
    halves = inverse.reshape(feat_count // 2, out_width, full_width)
    outgoing = jnp.concatenate([halves] * 2, axis=0)
    factor_rows = lax.all_to_all(outgoing, "feat", split_axis=0, concat_axis=0, tiled=True)
    parity = feat * out_width // full_width
    scalars = jnp.concatenate([parity[None].astype(jnp.int32), low, high, places])
    return whiten(scalars, pairs, factor_rows)


def solution(mesh):
    return jax.shard_map(
        shards,
        mesh=mesh,
        in_specs=(P("bank", "feat"), P()),
        out_specs=P("bank", "feat"),
        check_vma=False,
    )
```

```python
import functools

import jax
import jax.numpy as jnp
from jax import lax
from jax.experimental import pallas as pl
from jax.experimental.pallas import tpu as pltpu
from jax.sharding import PartitionSpec as P

TOUCH = 4
BLOCK = 128
SUB = 8
ridge_shift = 0.5


MESH = pl.DeviceIdType.MESH
GATHER_CHUNKS = 4


def slot_of(offsets, role, row_start, rows_dev):
    clusters = offsets.shape[0] - 1

    def count(k, found):
        bound = offsets[k]
        first, last = found
        first = first + (bound <= row_start).astype(jnp.int32)
        last = last + (bound <= row_start + rows_dev - 1).astype(jnp.int32)
        return first, last

    first, last = lax.fori_loop(1, clusters, count, (jnp.int32(0), jnp.int32(0)))
    is_last = role == TOUCH - 1
    label = jnp.where(is_last, last, jnp.minimum(first + role, last))
    used = jnp.logical_or(is_last, first + role < last)
    low = jnp.clip(offsets[label] - row_start, 0, rows_dev)
    high = jnp.clip(offsets[label + 1] - row_start, 0, rows_dev)
    return low, jnp.where(used, high, low), label


def own_role():
    feat = lax.axis_index("feat")
    return jnp.where(lax.axis_index("bank") % 2 == 0, feat, TOUCH - 1 - feat)


def neighbours():
    bank, feat = lax.axis_index("bank"), lax.axis_index("feat")
    sibling = feat + 1 - 2 * (feat % 2)
    return bank, sibling, (feat + 2) % TOUCH, (sibling + 2) % TOUCH


def greet(bank, others):
    barrier = pltpu.get_barrier_semaphore()
    for other in others:
        pl.semaphore_signal(barrier, inc=1, device_id=(bank, other), device_id_type=MESH)
    pl.semaphore_wait(barrier, len(others))


def gather_kernel(own, near, across, far, send, receive):
    bank, sibling, partner, _ = neighbours()
    greet(bank, (sibling, partner))
    piece = own.shape[0] // GATHER_CHUNKS

    def remote(source, target, place, device):
        return pltpu.make_async_remote_copy(
            src_ref=source,
            dst_ref=target,
            send_sem=send.at[place],
            recv_sem=receive.at[place],
            device_id=(bank, device),
            device_id_type=MESH,
        )

    firsts, seconds = [], []
    for i in range(GATHER_CHUNKS):
        span = pl.ds(i * piece, piece)
        firsts.append(remote(own.at[span, :], across.at[span, :], i, partner))
        seconds.append(
            remote(across.at[span, :], far.at[span, :], GATHER_CHUNKS + i, sibling)
        )
    beside = remote(own, near, 2 * GATHER_CHUNKS, sibling)
    for copy in firsts:
        copy.start()
    beside.start()
    for first, second in zip(firsts, seconds):
        first.wait_recv()
        second.start()
    for copy in firsts:
        copy.wait_send()
    for copy in seconds:
        copy.wait()
    beside.wait()


def gather_rows(own):
    anywhere = pl.BlockSpec(memory_space=pl.ANY)
    return pl.pallas_call(
        gather_kernel,
        in_specs=[anywhere],
        out_specs=[anywhere] * 3,
        out_shape=[jax.ShapeDtypeStruct(own.shape, own.dtype)] * 3,
        scratch_shapes=[
            pltpu.SemaphoreType.DMA((2 * GATHER_CHUNKS + 1,)),
            pltpu.SemaphoreType.DMA((2 * GATHER_CHUNKS + 1,)),
        ],
        compiler_params=pltpu.CompilerParams(collective_id=0, has_side_effects=True),
    )(own)


def upper_blocks(width):
    blocks = width // BLOCK
    return [(i, k) for i in range(blocks) for k in range(i, blocks)]


def ordered(first, second, swap):
    left = jnp.where(swap, second, first)
    right = jnp.where(swap, first, second)
    return jnp.concatenate([left, right], axis=1)


def gram_kernel(offsets, own, near, across, far, packed_ref, gram):
    step = pl.program_id(0)
    block_pairs = own.shape[0]
    rows_dev = pl.num_programs(0) * block_pairs * 2
    low, high, _ = slot_of(offsets, own_role(), lax.axis_index("bank") * rows_dev, rows_dev)
    start = step * block_pairs * 2
    feat = lax.axis_index("feat")
    swap = feat % 2 == 1
    parity = feat // 2

    @pl.when(step == 0)
    def _():
        gram[...] = jnp.zeros_like(gram)

    @pl.when(jnp.logical_and(start < high, start + 2 * block_pairs > low))
    def _():
        row = start + 2 * lax.broadcasted_iota(jnp.int32, (block_pairs, 1), 0)
        for first, second, shift in ((own, near, parity), (across, far, 1 - parity)):
            data = ordered(first[...], second[...], swap)
            keep = jnp.logical_and(row + shift >= low, row + shift < high)
            data = jnp.where(keep, data, jnp.zeros_like(data))
            gram[...] += lax.dot_general(
                data, data, (((0,), (0,)), ((), ())), preferred_element_type=jnp.float32
            )

    @pl.when(step == pl.num_programs(0) - 1)
    def _():
        for place, (i, k) in enumerate(upper_blocks(gram.shape[0])):
            packed_ref[place] = gram[i * BLOCK : (i + 1) * BLOCK, k * BLOCK : (k + 1) * BLOCK]


def own_gram(offsets, own, near, across, far):
    pair_rows, half = own.shape
    width = 2 * half
    block_pairs = min(256, pair_rows)
    packed = (len(upper_blocks(width)), BLOCK, BLOCK)
    return pl.pallas_call(
        gram_kernel,
        grid=(pair_rows // block_pairs,),
        in_specs=[pl.BlockSpec(memory_space=pltpu.SMEM)]
        + [pl.BlockSpec((block_pairs, half), lambda i: (i, 0))] * 4,
        out_specs=pl.BlockSpec(packed, lambda i: (0, 0, 0)),
        out_shape=jax.ShapeDtypeStruct(packed, jnp.float32),
        scratch_shapes=[pltpu.VMEM((width, width), jnp.float32)],
        compiler_params=pltpu.CompilerParams(vmem_limit_bytes=32 << 20),
    )(offsets, own, near, across, far)


def split_rows(value):
    high = value.astype(jnp.bfloat16).astype(jnp.float32)
    rest = value - high
    middle = rest.astype(jnp.bfloat16).astype(jnp.float32)
    low = (rest - middle).astype(jnp.bfloat16).astype(jnp.float32)
    return high, middle, low


def factor_block(work):
    for panel in range(BLOCK // SUB):
        base = panel * SUB
        rows = [work[base + i : base + i + 1, :] for i in range(SUB)]
        entry = {}
        for i in range(SUB):
            for k in range(i, SUB):
                column = base + k
                entry[i, k] = jnp.broadcast_to(rows[i][:, column : column + 1], (1, BLOCK))
        done = []
        for i in range(SUB):
            inverse_root = lax.rsqrt(entry[i, i])
            coefficient = {k: entry[i, k] * inverse_root for k in range(i + 1, SUB)}
            for k in range(i + 1, SUB):
                for m in range(k, SUB):
                    entry[k, m] = entry[k, m] - coefficient[k] * coefficient[m]
            scaled = rows[i] * jnp.concatenate([inverse_root, inverse_root], axis=1)
            done.append(scaled)
            for k in range(i + 1, SUB):
                both = jnp.concatenate([coefficient[k], coefficient[k]], axis=1)
                rows[k] = rows[k] - both * scaled
        for i in range(SUB):
            work[base + i : base + i + 1, :] = done[i]
        if base + SUB < BLOCK:
            high, middle, low = split_rows(work[base : base + SUB, :])
            left = jnp.concatenate([high, high, middle, high, middle, low], axis=0)
            right = jnp.concatenate([high, middle, high, low, middle, high], axis=0)
            update = lax.dot_general(
                left[:, :BLOCK].astype(jnp.bfloat16),
                right.astype(jnp.bfloat16),
                (((0,), (0,)), ((), ())),
                preferred_element_type=jnp.float32,
            )
            work[base + SUB :, :] = work[base + SUB :, :] - update[base + SUB :, :]


def whitener_kernel(rows_dev, offsets, own_ref, other_ref, out_ref, matrix, work):
    width = out_ref.shape[0]
    blocks = width // BLOCK
    role = own_role()
    row_start = lax.axis_index("bank") * rows_dev
    _, _, label = slot_of(offsets, role, row_start, rows_dev)
    left_open = jnp.logical_and(role == 0, offsets[label] < row_start)
    right_open = jnp.logical_and(role == TOUCH - 1, offsets[label + 1] > row_start + rows_dev)
    joined = jnp.logical_or(left_open, right_open)
    count = (offsets[label + 1] - offsets[label]).astype(jnp.float32)
    eye = (
        lax.broadcasted_iota(jnp.int32, (BLOCK, BLOCK), 0)
        == lax.broadcasted_iota(jnp.int32, (BLOCK, BLOCK), 1)
    ).astype(jnp.float32)
    for place, (i, k) in enumerate(upper_blocks(width)):
        total = own_ref[place] + jnp.where(joined, other_ref[place], 0.0)
        total = total / count
        if i == k:
            total = total + ridge_shift * eye
        else:
            matrix[k * BLOCK : (k + 1) * BLOCK, i * BLOCK : (i + 1) * BLOCK] = jnp.zeros_like(eye)
        matrix[i * BLOCK : (i + 1) * BLOCK, k * BLOCK : (k + 1) * BLOCK] = total

    @pl.loop(0, blocks)
    def _(j):
        here = pl.ds(pl.multiple_of(j * BLOCK, BLOCK), BLOCK)
        work[:, :BLOCK] = matrix[here, here]
        work[:, BLOCK:] = eye
        factor_block(work)
        matrix[here, here] = eye
        panel = lax.dot_general(
            work[:, BLOCK:],
            matrix[here, :],
            (((1,), (0,)), ((), ())),
            precision=lax.Precision.HIGHEST,
            preferred_element_type=jnp.float32,
        )
        matrix[here, :] = panel

        @pl.loop(j + 1, blocks)
        def _(i):
            there = pl.ds(pl.multiple_of(i * BLOCK, BLOCK), BLOCK)
            update = lax.dot_general(
                matrix[here, there],
                matrix[here, :],
                (((0,), (0,)), ((), ())),
                precision=lax.Precision.HIGHEST,
                preferred_element_type=jnp.float32,
            )
            matrix[there, here] = jnp.zeros_like(eye)
            matrix[there, :] = matrix[there, :] - update

        column = lax.broadcasted_iota(jnp.int32, (BLOCK, width), 1)
        final = jnp.where(column < (j + 1) * BLOCK, matrix[here, :], 0.0)
        out_ref[here, :] = final.astype(jnp.bfloat16)


def own_whitener(rows_dev, width, offsets, own, other):
    return pl.pallas_call(
        functools.partial(whitener_kernel, rows_dev),
        in_specs=[
            pl.BlockSpec(memory_space=pltpu.SMEM),
            pl.BlockSpec(memory_space=pltpu.VMEM),
            pl.BlockSpec(memory_space=pltpu.VMEM),
        ],
        out_specs=pl.BlockSpec(memory_space=pltpu.VMEM),
        out_shape=jax.ShapeDtypeStruct((width, width), jnp.bfloat16),
        scratch_shapes=[
            pltpu.VMEM((width, width), jnp.float32),
            pltpu.VMEM((BLOCK, 2 * BLOCK), jnp.float32),
        ],
        compiler_params=pltpu.CompilerParams(vmem_limit_bytes=32 << 20),
    )(offsets, own, other)


def spread_kernel(whitener, rows_ref, send, receive, local):
    bank, sibling, partner, diagonal = neighbours()
    feat = lax.axis_index("feat")
    half = rows_ref.shape[1]
    strips = half // BLOCK
    greet(bank, (sibling, partner, diagonal))

    def copies(place, device, upper):
        made = []
        for i in range(strips):
            first = (0 if upper else half) + i * BLOCK
            columns = pl.ds(0, first + BLOCK)
            made.append(
                pltpu.make_async_remote_copy(
                    src_ref=whitener.at[pl.ds(first, BLOCK), columns],
                    dst_ref=rows_ref.at[feat, pl.ds(i * BLOCK, BLOCK), columns],
                    send_sem=send.at[place, i],
                    recv_sem=receive.at[place, i],
                    device_id=(bank, device),
                    device_id_type=MESH,
                )
            )
        return made

    for upper_mine in (True, False):

        @pl.when(feat % 2 == (0 if upper_mine else 1))
        def _():
            sent = (
                copies(0, partner, upper_mine)
                + copies(1, diagonal, not upper_mine)
                + copies(2, sibling, not upper_mine)
            )
            for copy in sent:
                copy.start()
            source = whitener.at[pl.ds(0 if upper_mine else half, half), :]
            stay = pltpu.make_async_copy(source, rows_ref.at[feat], local)
            stay.start()
            for copy in sent:
                copy.wait_send()
            stay.wait()
            got = (
                copies(0, partner, upper_mine)
                + copies(1, diagonal, upper_mine)
                + copies(2, sibling, upper_mine)
            )
            for copy in got:
                copy.wait_recv()


def spread(whitener):
    width = whitener.shape[0]
    half = width // 2
    anywhere = pl.BlockSpec(memory_space=pl.ANY)
    return pl.pallas_call(
        spread_kernel,
        in_specs=[anywhere],
        out_specs=anywhere,
        out_shape=jax.ShapeDtypeStruct((TOUCH, half, width), whitener.dtype),
        scratch_shapes=[
            pltpu.SemaphoreType.DMA((3, half // BLOCK)),
            pltpu.SemaphoreType.DMA((3, half // BLOCK)),
            pltpu.SemaphoreType.DMA,
        ],
        compiler_params=pltpu.CompilerParams(collective_id=1, has_side_effects=True),
    )(whitener)


def whiten_kernel(offsets, own, near, factor_ref, out_ref, factors, total):
    step = pl.program_id(0)
    block_pairs, half = own.shape
    rows_dev = pl.num_programs(0) * block_pairs * 2
    bank, feat = lax.axis_index("bank"), lax.axis_index("feat")
    start = step * block_pairs * 2

    @pl.when(step == 0)
    def _():
        shape = factor_ref.shape[1:]
        row = (feat % 2) * half + lax.broadcasted_iota(jnp.int32, shape, 0)
        inside = lax.broadcasted_iota(jnp.int32, shape, 1) <= row
        for place in range(TOUCH):
            rows = factor_ref[place]
            factors[place] = jnp.where(inside, rows, jnp.zeros_like(rows))

    total[...] = jnp.zeros_like(total)
    for role in range(TOUCH):
        low, high, _ = slot_of(offsets, jnp.int32(role), bank * rows_dev, rows_dev)

        @pl.when(jnp.logical_and(start < high, start + 2 * block_pairs > low))
        def _():
            place = jnp.where(bank % 2 == 0, role, TOUCH - 1 - role)
            row = start + feat // 2 + 2 * lax.broadcasted_iota(jnp.int32, (block_pairs, 1), 0)
            data = ordered(own[...], near[...], feat % 2 == 1)
            keep = jnp.logical_and(row >= low, row < high)
            data = jnp.where(keep, data, jnp.zeros_like(data))
            total[...] += lax.dot_general(
                data, factors[place], (((1,), (1,)), ((), ())), preferred_element_type=jnp.float32
            )

    out_ref[...] = total[...].astype(jnp.bfloat16)


def whiten(offsets, own, near, factor_rows):
    pair_rows, half = own.shape
    block_pairs = min(256, pair_rows)
    block = pl.BlockSpec((block_pairs, half), lambda i: (i, 0))
    return pl.pallas_call(
        whiten_kernel,
        grid=(pair_rows // block_pairs,),
        in_specs=[
            pl.BlockSpec(memory_space=pltpu.SMEM),
            block,
            block,
            pl.BlockSpec(factor_rows.shape, lambda i: (0, 0, 0)),
        ],
        out_specs=block,
        out_shape=jax.ShapeDtypeStruct((pair_rows, half), jnp.bfloat16),
        scratch_shapes=[
            pltpu.VMEM(factor_rows.shape, jnp.bfloat16),
            pltpu.VMEM((block_pairs, half), jnp.float32),
        ],
        compiler_params=pltpu.CompilerParams(vmem_limit_bytes=32 << 20),
    )(offsets, own, near, factor_rows)


def meeting_pairs(bank_count, feat_count):
    pairs = []
    for bank in range(bank_count - 1):
        place = feat_count - 1 if bank % 2 == 0 else 0
        left, right = bank * feat_count + place, (bank + 1) * feat_count + place
        pairs += [(left, right), (right, left)]
    return pairs


def shards(bank_rows, offsets):
    pair_rows, out_width = bank_rows.shape
    near, across, far = gather_rows(bank_rows)
    own = own_gram(offsets, bank_rows, near, across, far)
    pairs = meeting_pairs(lax.axis_size("bank"), lax.axis_size("feat"))
    other = lax.ppermute(own, ("bank", "feat"), pairs)
    inverse = own_whitener(pair_rows * 2, 2 * out_width, offsets, own, other)
    return whiten(offsets, bank_rows, near, spread(inverse))


def solution(mesh):
    return jax.shard_map(
        shards,
        mesh=mesh,
        in_specs=(P("bank", "feat"), P()),
        out_specs=P("bank", "feat"),
        check_vma=False,
    )
```

```python
import functools

import jax
import jax.numpy as jnp
from jax import lax
from jax.experimental import pallas as pl
from jax.experimental.pallas import tpu as pltpu
from jax.sharding import PartitionSpec as P

TOUCH = 4
BLOCK = 128
SUB = 8
ridge_shift = 0.5


MESH = pl.DeviceIdType.MESH
GATHER_CHUNKS = 4


def slot_of(offsets, role, row_start, rows_dev):
    clusters = offsets.shape[0] - 1

    def count(k, found):
        bound = offsets[k]
        first, last = found
        first = first + (bound <= row_start).astype(jnp.int32)
        last = last + (bound <= row_start + rows_dev - 1).astype(jnp.int32)
        return first, last

    first, last = lax.fori_loop(1, clusters, count, (jnp.int32(0), jnp.int32(0)))
    is_last = role == TOUCH - 1
    label = jnp.where(is_last, last, jnp.minimum(first + role, last))
    used = jnp.logical_or(is_last, first + role < last)
    low = jnp.clip(offsets[label] - row_start, 0, rows_dev)
    high = jnp.clip(offsets[label + 1] - row_start, 0, rows_dev)
    return low, jnp.where(used, high, low), label


def own_role():
    feat = lax.axis_index("feat")
    return jnp.where(lax.axis_index("bank") % 2 == 0, feat, TOUCH - 1 - feat)


def neighbours():
    bank, feat = lax.axis_index("bank"), lax.axis_index("feat")
    sibling = feat + 1 - 2 * (feat % 2)
    return bank, sibling, (feat + 2) % TOUCH, (sibling + 2) % TOUCH


def greet(bank, others):
    barrier = pltpu.get_barrier_semaphore()
    for other in others:
        pl.semaphore_signal(barrier, inc=1, device_id=(bank, other), device_id_type=MESH)
    pl.semaphore_wait(barrier, len(others))


def gather_kernel(own, near, across, far, send, receive):
    bank, sibling, partner, _ = neighbours()
    greet(bank, (sibling, partner))
    piece = own.shape[0] // GATHER_CHUNKS

    def remote(source, target, place, device):
        return pltpu.make_async_remote_copy(
            src_ref=source,
            dst_ref=target,
            send_sem=send.at[place],
            recv_sem=receive.at[place],
            device_id=(bank, device),
            device_id_type=MESH,
        )

    firsts, seconds = [], []
    for i in range(GATHER_CHUNKS):
        span = pl.ds(i * piece, piece)
        firsts.append(remote(own.at[span, :], across.at[span, :], i, partner))
        seconds.append(
            remote(across.at[span, :], far.at[span, :], GATHER_CHUNKS + i, sibling)
        )
    beside = remote(own, near, 2 * GATHER_CHUNKS, sibling)
    for copy in firsts:
        copy.start()
    beside.start()
    for first, second in zip(firsts, seconds):
        first.wait_recv()
        second.start()
    for copy in firsts:
        copy.wait_send()
    for copy in seconds:
        copy.wait()
    beside.wait()


def gather_rows(own):
    anywhere = pl.BlockSpec(memory_space=pl.ANY)
    return pl.pallas_call(
        gather_kernel,
        in_specs=[anywhere],
        out_specs=[anywhere] * 3,
        out_shape=[jax.ShapeDtypeStruct(own.shape, own.dtype)] * 3,
        scratch_shapes=[
            pltpu.SemaphoreType.DMA((2 * GATHER_CHUNKS + 1,)),
            pltpu.SemaphoreType.DMA((2 * GATHER_CHUNKS + 1,)),
        ],
        compiler_params=pltpu.CompilerParams(collective_id=0, has_side_effects=True),
    )(own)


def upper_blocks(width):
    blocks = width // BLOCK
    return [(i, k) for i in range(blocks) for k in range(i, blocks)]


def ordered(first, second, swap):
    left = jnp.where(swap, second, first)
    right = jnp.where(swap, first, second)
    return jnp.concatenate([left, right], axis=1)


def gram_kernel(offsets, own, near, across, far, packed_ref, gram):
    step = pl.program_id(0)
    block_pairs = own.shape[0]
    rows_dev = pl.num_programs(0) * block_pairs * 2
    low, high, _ = slot_of(offsets, own_role(), lax.axis_index("bank") * rows_dev, rows_dev)
    start = step * block_pairs * 2
    feat = lax.axis_index("feat")
    swap = feat % 2 == 1
    parity = feat // 2

    @pl.when(step == 0)
    def _():
        gram[...] = jnp.zeros_like(gram)

    @pl.when(jnp.logical_and(start < high, start + 2 * block_pairs > low))
    def _():
        row = start + 2 * lax.broadcasted_iota(jnp.int32, (block_pairs, 1), 0)
        for first, second, shift in ((own, near, parity), (across, far, 1 - parity)):
            data = ordered(first[...], second[...], swap)
            keep = jnp.logical_and(row + shift >= low, row + shift < high)
            data = jnp.where(keep, data, jnp.zeros_like(data))
            gram[...] += lax.dot_general(
                data, data, (((0,), (0,)), ((), ())), preferred_element_type=jnp.float32
            )

    @pl.when(step == pl.num_programs(0) - 1)
    def _():
        for place, (i, k) in enumerate(upper_blocks(gram.shape[0])):
            packed_ref[place] = gram[i * BLOCK : (i + 1) * BLOCK, k * BLOCK : (k + 1) * BLOCK]


def own_gram(offsets, own, near, across, far):
    pair_rows, half = own.shape
    width = 2 * half
    block_pairs = min(256, pair_rows)
    packed = (len(upper_blocks(width)), BLOCK, BLOCK)
    return pl.pallas_call(
        gram_kernel,
        grid=(pair_rows // block_pairs,),
        in_specs=[pl.BlockSpec(memory_space=pltpu.SMEM)]
        + [pl.BlockSpec((block_pairs, half), lambda i: (i, 0))] * 4,
        out_specs=pl.BlockSpec(packed, lambda i: (0, 0, 0)),
        out_shape=jax.ShapeDtypeStruct(packed, jnp.float32),
        scratch_shapes=[pltpu.VMEM((width, width), jnp.float32)],
        compiler_params=pltpu.CompilerParams(vmem_limit_bytes=32 << 20),
    )(offsets, own, near, across, far)


def split_rows(value):
    high = value.astype(jnp.bfloat16).astype(jnp.float32)
    rest = value - high
    middle = rest.astype(jnp.bfloat16).astype(jnp.float32)
    low = (rest - middle).astype(jnp.bfloat16).astype(jnp.float32)
    return high, middle, low


def factor_block(work):
    for panel in range(BLOCK // SUB):
        base = panel * SUB
        rows = [work[base + i : base + i + 1, :] for i in range(SUB)]
        entry = {}
        for i in range(SUB):
            for k in range(i, SUB):
                column = base + k
                entry[i, k] = jnp.broadcast_to(rows[i][:, column : column + 1], (1, BLOCK))
        done = []
        for i in range(SUB):
            inverse_root = lax.rsqrt(entry[i, i])
            coefficient = {k: entry[i, k] * inverse_root for k in range(i + 1, SUB)}
            for k in range(i + 1, SUB):
                for m in range(k, SUB):
                    entry[k, m] = entry[k, m] - coefficient[k] * coefficient[m]
            scaled = rows[i] * jnp.concatenate([inverse_root, inverse_root], axis=1)
            done.append(scaled)
            for k in range(i + 1, SUB):
                both = jnp.concatenate([coefficient[k], coefficient[k]], axis=1)
                rows[k] = rows[k] - both * scaled
        for i in range(SUB):
            work[base + i : base + i + 1, :] = done[i]
        if base + SUB < BLOCK:
            high, middle, low = split_rows(work[base : base + SUB, :])
            left = jnp.concatenate([high, high, middle, high, middle, low], axis=0)
            right = jnp.concatenate([high, middle, high, low, middle, high], axis=0)
            update = lax.dot_general(
                left[:, :BLOCK].astype(jnp.bfloat16),
                right.astype(jnp.bfloat16),
                (((0,), (0,)), ((), ())),
                preferred_element_type=jnp.float32,
            )
            work[base + SUB :, :] = work[base + SUB :, :] - update[base + SUB :, :]


def whitener_kernel(
    rows_dev, bank_count, offsets, own_ref, rows_ref, other, matrix, work, final,
    swap_send, swap_receive, send, receive, local,
):
    width = matrix.shape[0]
    half = width // 2
    blocks = width // BLOCK
    strips = half // BLOCK
    bank, sibling, partner, diagonal = neighbours()
    feat = lax.axis_index("feat")
    role = own_role()
    meets_left = jnp.logical_and(role == 0, bank > 0)
    meets_right = jnp.logical_and(role == TOUCH - 1, bank < bank_count - 1)
    meets = jnp.logical_or(meets_left, meets_right)
    met = jnp.where(meets_left, bank - 1, bank + 1)

    barrier = pltpu.get_barrier_semaphore()
    for device in (sibling, partner, diagonal):
        pl.semaphore_signal(barrier, inc=1, device_id=(bank, device), device_id_type=MESH)

    def swap(i):
        place = sum(blocks - k for k in range(i))
        span = pl.ds(place, blocks - i)
        return pltpu.make_async_remote_copy(
            src_ref=own_ref.at[span],
            dst_ref=other.at[span],
            send_sem=swap_send.at[i],
            recv_sem=swap_receive.at[i],
            device_id=(met, feat),
            device_id_type=MESH,
        )

    @pl.when(meets)
    def _():
        pl.semaphore_signal(barrier, inc=1, device_id=(met, feat), device_id_type=MESH)
        pl.semaphore_wait(barrier, 4)
        for i in range(blocks):
            swap(i).start()

    @pl.when(jnp.logical_not(meets))
    def _():
        pl.semaphore_wait(barrier, 3)
        other[...] = jnp.zeros_like(other)

    row_start = bank * rows_dev
    _, _, label = slot_of(offsets, role, row_start, rows_dev)
    left_open = jnp.logical_and(role == 0, offsets[label] < row_start)
    right_open = jnp.logical_and(role == TOUCH - 1, offsets[label + 1] > row_start + rows_dev)
    joined = jnp.logical_or(left_open, right_open)
    count = (offsets[label + 1] - offsets[label]).astype(jnp.float32)
    eye = (
        lax.broadcasted_iota(jnp.int32, (BLOCK, BLOCK), 0)
        == lax.broadcasted_iota(jnp.int32, (BLOCK, BLOCK), 1)
    ).astype(jnp.float32)

    def strip(place, i, device):
        columns = pl.ds(0, (i + 1) * BLOCK)
        return pltpu.make_async_remote_copy(
            src_ref=final.at[pl.ds(i * BLOCK, BLOCK), columns],
            dst_ref=rows_ref.at[feat, pl.ds(i % strips * BLOCK, BLOCK), columns],
            send_sem=send.at[place, i % strips],
            recv_sem=receive.at[place, i % strips],
            device_id=(bank, device),
            device_id_type=MESH,
        )

    def stay(i):
        columns = pl.ds(0, (i + 1) * BLOCK)
        return pltpu.make_async_copy(
            final.at[pl.ds(i * BLOCK, BLOCK), columns],
            rows_ref.at[feat, pl.ds(i % strips * BLOCK, BLOCK), columns],
            local.at[i % strips],
        )

    @pl.loop(0, blocks)
    def _(j):
        here = pl.ds(pl.multiple_of(j * BLOCK, BLOCK), BLOCK)
        for i in range(blocks):

            @pl.when(j == i)
            def _():
                @pl.when(meets)
                def _():
                    swap(i).wait_recv()

                for k in range(i, blocks):
                    place = sum(blocks - n for n in range(i)) + k - i
                    total = own_ref[place] + jnp.where(joined, other[place], 0.0)
                    total = total / count
                    if i == k:
                        total = total + ridge_shift * eye
                    matrix[i * BLOCK : (i + 1) * BLOCK, k * BLOCK : (k + 1) * BLOCK] = total

        @pl.loop(0, j)
        def _(k):
            above = pl.ds(pl.multiple_of(k * BLOCK, BLOCK), BLOCK)
            update = lax.dot_general(
                matrix[above, here],
                matrix[above, :],
                (((0,), (0,)), ((), ())),
                precision=lax.Precision.HIGHEST,
                preferred_element_type=jnp.float32,
            )
            matrix[here, above] = jnp.zeros_like(eye)
            matrix[here, :] = matrix[here, :] - update

        work[:, :BLOCK] = matrix[here, here]
        work[:, BLOCK:] = eye
        factor_block(work)
        matrix[here, here] = eye
        panel = lax.dot_general(
            work[:, BLOCK:],
            matrix[here, :],
            (((1,), (0,)), ((), ())),
            precision=lax.Precision.HIGHEST,
            preferred_element_type=jnp.float32,
        )
        matrix[here, :] = panel
        final[here, :] = panel.astype(jnp.bfloat16)
        for i in range(blocks):
            mine = 0 if i < strips else 1

            @pl.when(jnp.logical_and(j == i, feat % 2 == mine))
            def _():
                strip(0, i, partner).start()
                stay(i).start()

            @pl.when(jnp.logical_and(j == i, feat % 2 != mine))
            def _():
                strip(1, i, diagonal).start()
                strip(2, i, sibling).start()

    @pl.when(meets)
    def _():
        for i in range(blocks):
            swap(i).wait_send()

    for parity in range(2):

        @pl.when(feat % 2 == parity)
        def _():
            for i in range(strips):
                mine, others = parity * strips + i, (1 - parity) * strips + i
                strip(0, mine, partner).wait_send()
                strip(1, others, diagonal).wait_send()
                strip(2, others, sibling).wait_send()
                stay(mine).wait()
            for i in range(strips):
                mine = parity * strips + i
                strip(0, mine, partner).wait_recv()
                strip(1, mine, diagonal).wait_recv()
                strip(2, mine, sibling).wait_recv()


def whitener_rows(rows_dev, width, offsets, own):
    half, blocks = width // 2, width // BLOCK
    strips = half // BLOCK
    return pl.pallas_call(
        functools.partial(whitener_kernel, rows_dev, lax.axis_size("bank")),
        in_specs=[
            pl.BlockSpec(memory_space=pltpu.SMEM),
            pl.BlockSpec(memory_space=pltpu.VMEM),
        ],
        out_specs=pl.BlockSpec(memory_space=pl.ANY),
        out_shape=jax.ShapeDtypeStruct((TOUCH, half, width), jnp.bfloat16),
        scratch_shapes=[
            pltpu.VMEM(own.shape, jnp.float32),
            pltpu.VMEM((width, width), jnp.float32),
            pltpu.VMEM((BLOCK, 2 * BLOCK), jnp.float32),
            pltpu.VMEM((width, width), jnp.bfloat16),
            pltpu.SemaphoreType.DMA((blocks,)),
            pltpu.SemaphoreType.DMA((blocks,)),
            pltpu.SemaphoreType.DMA((3, strips)),
            pltpu.SemaphoreType.DMA((3, strips)),
            pltpu.SemaphoreType.DMA((strips,)),
        ],
        compiler_params=pltpu.CompilerParams(
            collective_id=1, has_side_effects=True, vmem_limit_bytes=32 << 20
        ),
    )(offsets, own)


def whiten_kernel(offsets, own, near, factor_ref, out_ref, factors, total):
    step = pl.program_id(0)
    block_pairs, half = own.shape
    rows_dev = pl.num_programs(0) * block_pairs * 2
    bank, feat = lax.axis_index("bank"), lax.axis_index("feat")
    start = step * block_pairs * 2

    @pl.when(step == 0)
    def _():
        shape = factor_ref.shape[1:]
        row = (feat % 2) * half + lax.broadcasted_iota(jnp.int32, shape, 0)
        inside = lax.broadcasted_iota(jnp.int32, shape, 1) <= row
        for place in range(TOUCH):
            rows = factor_ref[place]
            factors[place] = jnp.where(inside, rows, jnp.zeros_like(rows))

    total[...] = jnp.zeros_like(total)
    for role in range(TOUCH):
        low, high, _ = slot_of(offsets, jnp.int32(role), bank * rows_dev, rows_dev)

        @pl.when(jnp.logical_and(start < high, start + 2 * block_pairs > low))
        def _():
            place = jnp.where(bank % 2 == 0, role, TOUCH - 1 - role)
            row = start + feat // 2 + 2 * lax.broadcasted_iota(jnp.int32, (block_pairs, 1), 0)
            data = ordered(own[...], near[...], feat % 2 == 1)
            keep = jnp.logical_and(row >= low, row < high)
            data = jnp.where(keep, data, jnp.zeros_like(data))
            total[...] += lax.dot_general(
                data, factors[place], (((1,), (1,)), ((), ())), preferred_element_type=jnp.float32
            )

    out_ref[...] = total[...].astype(jnp.bfloat16)


def whiten(offsets, own, near, factor_rows):
    pair_rows, half = own.shape
    block_pairs = min(256, pair_rows)
    block = pl.BlockSpec((block_pairs, half), lambda i: (i, 0))
    return pl.pallas_call(
        whiten_kernel,
        grid=(pair_rows // block_pairs,),
        in_specs=[
            pl.BlockSpec(memory_space=pltpu.SMEM),
            block,
            block,
            pl.BlockSpec(factor_rows.shape, lambda i: (0, 0, 0)),
        ],
        out_specs=block,
        out_shape=jax.ShapeDtypeStruct((pair_rows, half), jnp.bfloat16),
        scratch_shapes=[
            pltpu.VMEM(factor_rows.shape, jnp.bfloat16),
            pltpu.VMEM((block_pairs, half), jnp.float32),
        ],
        compiler_params=pltpu.CompilerParams(vmem_limit_bytes=32 << 20),
    )(offsets, own, near, factor_rows)


def shards(bank_rows, offsets):
    pair_rows, out_width = bank_rows.shape
    near, across, far = gather_rows(bank_rows)
    own = own_gram(offsets, bank_rows, near, across, far)
    factor_rows = whitener_rows(pair_rows * 2, 2 * out_width, offsets, own)
    return whiten(offsets, bank_rows, near, factor_rows)


def solution(mesh):
    return jax.shard_map(
        shards,
        mesh=mesh,
        in_specs=(P("bank", "feat"), P()),
        out_specs=P("bank", "feat"),
        check_vma=False,
    )
```

```python
import functools

import jax
import jax.numpy as jnp
from jax import lax
from jax.experimental import pallas as pl
from jax.experimental.pallas import tpu as pltpu
from jax.sharding import PartitionSpec as P

TOUCH = 4
BLOCK = 128
SUB = 8
ridge_shift = 0.5


MESH = pl.DeviceIdType.MESH
GATHER_CHUNKS = 6


def slot_of(offsets, role, row_start, rows_dev):
    clusters = offsets.shape[0] - 1

    def count(k, found):
        bound = offsets[k]
        first, last = found
        first = first + (bound <= row_start).astype(jnp.int32)
        last = last + (bound <= row_start + rows_dev - 1).astype(jnp.int32)
        return first, last

    first, last = lax.fori_loop(1, clusters, count, (jnp.int32(0), jnp.int32(0)))
    is_last = role == TOUCH - 1
    label = jnp.where(is_last, last, jnp.minimum(first + role, last))
    used = jnp.logical_or(is_last, first + role < last)
    low = jnp.clip(offsets[label] - row_start, 0, rows_dev)
    high = jnp.clip(offsets[label + 1] - row_start, 0, rows_dev)
    return low, jnp.where(used, high, low), label


def own_role():
    feat = lax.axis_index("feat")
    return jnp.where(lax.axis_index("bank") % 2 == 0, feat, TOUCH - 1 - feat)


def neighbours():
    bank, feat = lax.axis_index("bank"), lax.axis_index("feat")
    sibling = feat + 1 - 2 * (feat % 2)
    return bank, sibling, (feat + 2) % TOUCH, (sibling + 2) % TOUCH


def greet(bank, others):
    barrier = pltpu.get_barrier_semaphore()
    for other in others:
        pl.semaphore_signal(barrier, inc=1, device_id=(bank, other), device_id_type=MESH)
    pl.semaphore_wait(barrier, len(others))


def upper_blocks(width):
    blocks = width // BLOCK
    return [(i, k) for i in range(blocks) for k in range(i, blocks)]


def ordered(first, second, swap):
    left = jnp.where(swap, second, first)
    right = jnp.where(swap, first, second)
    return jnp.concatenate([left, right], axis=1)


def gram_kernel(
    offsets, own, packed_ref, near_ref, kept, near, across, far, gram, send, receive, local
):
    bank, sibling, partner, _ = neighbours()
    greet(bank, (sibling, partner))
    pair_rows, half = own.shape
    piece = pair_rows // GATHER_CHUNKS
    rows_dev = 2 * pair_rows

    def remote(source, target, place, device):
        return pltpu.make_async_remote_copy(
            src_ref=source,
            dst_ref=target,
            send_sem=send.at[place],
            recv_sem=receive.at[place],
            device_id=(bank, device),
            device_id_type=MESH,
        )

    def part(i):
        return pl.ds(pl.multiple_of(i * piece, piece), piece)

    def crossing(i):
        return remote(own.at[part(i), :], across.at[part(i), :], i, partner)

    def passing(i):
        return remote(across.at[part(i), :], far.at[part(i), :], GATHER_CHUNKS + i, sibling)

    beside = remote(own, near, 2 * GATHER_CHUNKS, sibling)
    fetch = pltpu.make_async_copy(own, kept, local.at[0])
    keep_near = pltpu.make_async_copy(near, near_ref, local.at[1])
    beside.start()

    @pl.loop(0, GATHER_CHUNKS)
    def _(i):
        crossing(i).start()

    fetch.start()
    low, high, _ = slot_of(offsets, own_role(), bank * rows_dev, rows_dev)
    feat = lax.axis_index("feat")
    parity = feat // 2
    gram[...] = jnp.zeros_like(gram)

    def add(first, second, i, shift):
        data = ordered(first[part(i), :], second[part(i), :], feat % 2 == 1)
        row = 2 * (i * piece + lax.broadcasted_iota(jnp.int32, (piece, 1), 0)) + shift
        inside = jnp.logical_and(row >= low, row < high)
        data = jnp.where(inside, data, jnp.zeros_like(data))
        gram[...] += lax.dot_general(
            data, data, (((0,), (0,)), ((), ())), preferred_element_type=jnp.float32
        )

    fetch.wait()
    beside.wait_recv()
    keep_near.start()

    @pl.loop(0, GATHER_CHUNKS)
    def _(i):
        add(kept, near, i, parity)

    @pl.loop(0, GATHER_CHUNKS + 1)
    def _(i):
        @pl.when(i < GATHER_CHUNKS)
        def _():
            crossing(i).wait_recv()
            passing(i).start()

        @pl.when(i > 0)
        def _():
            passing(i - 1).wait_recv()
            add(across, far, i - 1, 1 - parity)

    for place, (i, k) in enumerate(upper_blocks(2 * half)):
        packed_ref[place] = gram[i * BLOCK : (i + 1) * BLOCK, k * BLOCK : (k + 1) * BLOCK]

    @pl.loop(0, GATHER_CHUNKS)
    def _(i):
        crossing(i).wait_send()
        passing(i).wait_send()

    beside.wait_send()
    keep_near.wait()


def own_gram(offsets, own):
    width = 2 * own.shape[1]
    packed = (len(upper_blocks(width)), BLOCK, BLOCK)
    anywhere = pl.BlockSpec(memory_space=pl.ANY)
    return pl.pallas_call(
        gram_kernel,
        in_specs=[pl.BlockSpec(memory_space=pltpu.SMEM), anywhere],
        out_specs=[pl.BlockSpec(memory_space=pltpu.VMEM), anywhere],
        out_shape=[
            jax.ShapeDtypeStruct(packed, jnp.float32),
            jax.ShapeDtypeStruct(own.shape, own.dtype),
        ],
        scratch_shapes=[pltpu.VMEM(own.shape, own.dtype)] * 4
        + [
            pltpu.VMEM((width, width), jnp.float32),
            pltpu.SemaphoreType.DMA((2 * GATHER_CHUNKS + 1,)),
            pltpu.SemaphoreType.DMA((2 * GATHER_CHUNKS + 1,)),
            pltpu.SemaphoreType.DMA((2,)),
        ],
        compiler_params=pltpu.CompilerParams(
            collective_id=0, has_side_effects=True, vmem_limit_bytes=32 << 20
        ),
    )(offsets, own)


def split_rows(value):
    high = value.astype(jnp.bfloat16).astype(jnp.float32)
    rest = value - high
    middle = rest.astype(jnp.bfloat16).astype(jnp.float32)
    low = (rest - middle).astype(jnp.bfloat16).astype(jnp.float32)
    return high, middle, low


def factor_block(work):
    for panel in range(BLOCK // SUB):
        base = panel * SUB
        rows = [work[base + i : base + i + 1, :] for i in range(SUB)]
        entry = {}
        for i in range(SUB):
            for k in range(i, SUB):
                column = base + k
                entry[i, k] = jnp.broadcast_to(rows[i][:, column : column + 1], (1, BLOCK))
        done = []
        for i in range(SUB):
            inverse_root = lax.rsqrt(entry[i, i])
            coefficient = {k: entry[i, k] * inverse_root for k in range(i + 1, SUB)}
            for k in range(i + 1, SUB):
                for m in range(k, SUB):
                    entry[k, m] = entry[k, m] - coefficient[k] * coefficient[m]
            scaled = rows[i] * jnp.concatenate([inverse_root, inverse_root], axis=1)
            done.append(scaled)
            for k in range(i + 1, SUB):
                both = jnp.concatenate([coefficient[k], coefficient[k]], axis=1)
                rows[k] = rows[k] - both * scaled
        for i in range(SUB):
            work[base + i : base + i + 1, :] = done[i]
        if base + SUB < BLOCK:
            high, middle, low = split_rows(work[base : base + SUB, :])
            left = jnp.concatenate([high, high, middle, high, middle, low], axis=0)
            right = jnp.concatenate([high, middle, high, low, middle, high], axis=0)
            update = lax.dot_general(
                left[:, :BLOCK].astype(jnp.bfloat16),
                right.astype(jnp.bfloat16),
                (((0,), (0,)), ((), ())),
                preferred_element_type=jnp.float32,
            )
            work[base + SUB :, :] = work[base + SUB :, :] - update[base + SUB :, :]


def whitener_kernel(
    rows_dev, bank_count, offsets, own_ref, rows_ref, other, matrix, work, final,
    swap_send, swap_receive, send, receive, local,
):
    width = matrix.shape[0]
    half = width // 2
    blocks = width // BLOCK
    strips = half // BLOCK
    bank, sibling, partner, diagonal = neighbours()
    feat = lax.axis_index("feat")
    role = own_role()
    meets_left = jnp.logical_and(role == 0, bank > 0)
    meets_right = jnp.logical_and(role == TOUCH - 1, bank < bank_count - 1)
    meets = jnp.logical_or(meets_left, meets_right)
    met = jnp.where(meets_left, bank - 1, bank + 1)

    barrier = pltpu.get_barrier_semaphore()
    for device in (sibling, partner, diagonal):
        pl.semaphore_signal(barrier, inc=1, device_id=(bank, device), device_id_type=MESH)

    def swap(i):
        place = sum(blocks - k for k in range(i))
        span = pl.ds(place, blocks - i)
        return pltpu.make_async_remote_copy(
            src_ref=own_ref.at[span],
            dst_ref=other.at[span],
            send_sem=swap_send.at[i],
            recv_sem=swap_receive.at[i],
            device_id=(met, feat),
            device_id_type=MESH,
        )

    @pl.when(meets)
    def _():
        pl.semaphore_signal(barrier, inc=1, device_id=(met, feat), device_id_type=MESH)
        pl.semaphore_wait(barrier, 4)
        for i in range(blocks):
            swap(i).start()

    @pl.when(jnp.logical_not(meets))
    def _():
        pl.semaphore_wait(barrier, 3)
        other[...] = jnp.zeros_like(other)

    row_start = bank * rows_dev
    _, _, label = slot_of(offsets, role, row_start, rows_dev)
    left_open = jnp.logical_and(role == 0, offsets[label] < row_start)
    right_open = jnp.logical_and(role == TOUCH - 1, offsets[label + 1] > row_start + rows_dev)
    joined = jnp.logical_or(left_open, right_open)
    count = (offsets[label + 1] - offsets[label]).astype(jnp.float32)
    eye = (
        lax.broadcasted_iota(jnp.int32, (BLOCK, BLOCK), 0)
        == lax.broadcasted_iota(jnp.int32, (BLOCK, BLOCK), 1)
    ).astype(jnp.float32)

    def strip(place, i, device):
        columns = pl.ds(0, (i + 1) * BLOCK)
        return pltpu.make_async_remote_copy(
            src_ref=final.at[pl.ds(i * BLOCK, BLOCK), columns],
            dst_ref=rows_ref.at[feat, pl.ds(i % strips * BLOCK, BLOCK), columns],
            send_sem=send.at[place, i % strips],
            recv_sem=receive.at[place, i % strips],
            device_id=(bank, device),
            device_id_type=MESH,
        )

    def stay(i):
        columns = pl.ds(0, (i + 1) * BLOCK)
        return pltpu.make_async_copy(
            final.at[pl.ds(i * BLOCK, BLOCK), columns],
            rows_ref.at[feat, pl.ds(i % strips * BLOCK, BLOCK), columns],
            local.at[i % strips],
        )

    @pl.loop(0, blocks)
    def _(j):
        here = pl.ds(pl.multiple_of(j * BLOCK, BLOCK), BLOCK)
        for i in range(blocks):

            @pl.when(j == i)
            def _():
                @pl.when(meets)
                def _():
                    swap(i).wait_recv()

                for k in range(i, blocks):
                    place = sum(blocks - n for n in range(i)) + k - i
                    total = own_ref[place] + jnp.where(joined, other[place], 0.0)
                    total = total / count
                    if i == k:
                        total = total + ridge_shift * eye
                    matrix[i * BLOCK : (i + 1) * BLOCK, k * BLOCK : (k + 1) * BLOCK] = total

        @pl.loop(0, j)
        def _(k):
            above = pl.ds(pl.multiple_of(k * BLOCK, BLOCK), BLOCK)
            update = lax.dot_general(
                matrix[above, here],
                matrix[above, :],
                (((0,), (0,)), ((), ())),
                precision=lax.Precision.HIGHEST,
                preferred_element_type=jnp.float32,
            )
            matrix[here, above] = jnp.zeros_like(eye)
            matrix[here, :] = matrix[here, :] - update

        work[:, :BLOCK] = matrix[here, here]
        work[:, BLOCK:] = eye
        factor_block(work)
        matrix[here, here] = eye
        panel = lax.dot_general(
            work[:, BLOCK:],
            matrix[here, :],
            (((1,), (0,)), ((), ())),
            precision=lax.Precision.HIGHEST,
            preferred_element_type=jnp.float32,
        )
        matrix[here, :] = panel
        final[here, :] = panel.astype(jnp.bfloat16)
        for i in range(blocks):
            mine = 0 if i < strips else 1

            @pl.when(jnp.logical_and(j == i, feat % 2 == mine))
            def _():
                strip(0, i, partner).start()
                stay(i).start()

            @pl.when(jnp.logical_and(j == i, feat % 2 != mine))
            def _():
                strip(1, i, diagonal).start()
                strip(2, i, sibling).start()

    @pl.when(meets)
    def _():
        for i in range(blocks):
            swap(i).wait_send()

    for parity in range(2):

        @pl.when(feat % 2 == parity)
        def _():
            for i in range(strips):
                mine, others = parity * strips + i, (1 - parity) * strips + i
                strip(0, mine, partner).wait_send()
                strip(1, others, diagonal).wait_send()
                strip(2, others, sibling).wait_send()
                stay(mine).wait()
            for i in range(strips):
                mine = parity * strips + i
                strip(0, mine, partner).wait_recv()
                strip(1, mine, diagonal).wait_recv()
                strip(2, mine, sibling).wait_recv()


def whitener_rows(rows_dev, width, offsets, own):
    half, blocks = width // 2, width // BLOCK
    strips = half // BLOCK
    return pl.pallas_call(
        functools.partial(whitener_kernel, rows_dev, lax.axis_size("bank")),
        in_specs=[
            pl.BlockSpec(memory_space=pltpu.SMEM),
            pl.BlockSpec(memory_space=pltpu.VMEM),
        ],
        out_specs=pl.BlockSpec(memory_space=pl.ANY),
        out_shape=jax.ShapeDtypeStruct((TOUCH, half, width), jnp.bfloat16),
        scratch_shapes=[
            pltpu.VMEM(own.shape, jnp.float32),
            pltpu.VMEM((width, width), jnp.float32),
            pltpu.VMEM((BLOCK, 2 * BLOCK), jnp.float32),
            pltpu.VMEM((width, width), jnp.bfloat16),
            pltpu.SemaphoreType.DMA((blocks,)),
            pltpu.SemaphoreType.DMA((blocks,)),
            pltpu.SemaphoreType.DMA((3, strips)),
            pltpu.SemaphoreType.DMA((3, strips)),
            pltpu.SemaphoreType.DMA((strips,)),
        ],
        compiler_params=pltpu.CompilerParams(
            collective_id=1, has_side_effects=True, vmem_limit_bytes=32 << 20
        ),
    )(offsets, own)


def whiten_kernel(offsets, own, near, factor_ref, out_ref, factors, total, bounds):
    step = pl.program_id(0)
    block_pairs, half = own.shape
    rows_dev = pl.num_programs(0) * block_pairs * 2
    bank, feat = lax.axis_index("bank"), lax.axis_index("feat")
    start = step * block_pairs * 2

    @pl.when(step == 0)
    def _():
        shape = factor_ref.shape[1:]
        row = (feat % 2) * half + lax.broadcasted_iota(jnp.int32, shape, 0)
        inside = lax.broadcasted_iota(jnp.int32, shape, 1) <= row
        for role in range(TOUCH):
            bounds[role], bounds[TOUCH + role], _ = slot_of(
                offsets, jnp.int32(role), bank * rows_dev, rows_dev
            )
        for place in range(TOUCH):
            rows = factor_ref[place]
            factors[place] = jnp.where(inside, rows, jnp.zeros_like(rows))

    total[...] = jnp.zeros_like(total)
    for role in range(TOUCH):
        low, high = bounds[role], bounds[TOUCH + role]

        @pl.when(jnp.logical_and(start < high, start + 2 * block_pairs > low))
        def _():
            place = jnp.where(bank % 2 == 0, role, TOUCH - 1 - role)
            row = start + feat // 2 + 2 * lax.broadcasted_iota(jnp.int32, (block_pairs, 1), 0)
            data = ordered(own[...], near[...], feat % 2 == 1)
            keep = jnp.logical_and(row >= low, row < high)
            data = jnp.where(keep, data, jnp.zeros_like(data))
            total[...] += lax.dot_general(
                data, factors[place], (((1,), (1,)), ((), ())), preferred_element_type=jnp.float32
            )

    out_ref[...] = total[...].astype(jnp.bfloat16)


def whiten(offsets, own, near, factor_rows):
    pair_rows, half = own.shape
    block_pairs = min(256, pair_rows)
    block = pl.BlockSpec((block_pairs, half), lambda i: (i, 0))
    return pl.pallas_call(
        whiten_kernel,
        grid=(pair_rows // block_pairs,),
        in_specs=[
            pl.BlockSpec(memory_space=pltpu.SMEM),
            block,
            block,
            pl.BlockSpec(factor_rows.shape, lambda i: (0, 0, 0)),
        ],
        out_specs=block,
        out_shape=jax.ShapeDtypeStruct((pair_rows, half), jnp.bfloat16),
        scratch_shapes=[
            pltpu.VMEM(factor_rows.shape, jnp.bfloat16),
            pltpu.VMEM((block_pairs, half), jnp.float32),
            pltpu.SMEM((2 * TOUCH,), jnp.int32),
        ],
        compiler_params=pltpu.CompilerParams(vmem_limit_bytes=32 << 20),
    )(offsets, own, near, factor_rows)


def shards(bank_rows, offsets):
    pair_rows, out_width = bank_rows.shape
    own, near = own_gram(offsets, bank_rows)
    factor_rows = whitener_rows(pair_rows * 2, 2 * out_width, offsets, own)
    return whiten(offsets, bank_rows, near, factor_rows)


def solution(mesh):
    return jax.shard_map(
        shards,
        mesh=mesh,
        in_specs=(P("bank", "feat"), P()),
        out_specs=P("bank", "feat"),
        check_vma=False,
    )
```
